32 devices in a mesh: seq: 8 (over z, y), tp: 4 (over x, core).
Axes of the slice: x: 2, y: 2, z: 4, core: 2. Of those that a mesh axis runs over, the one named last changes fastest.
Arguments:
- prefill_tokens: bfloat16 [4096, 2304], P('seq'), may hold values from -6 to 6
- decode_tokens: bfloat16 [64, 2304], P('seq'), may hold values from -6 to 6
- attention_gain: float32 [2304], replicated, may hold values from 0.5 to 1.5
- qkv_weight: bfloat16 [2304, 3, 2304], P(None, None, 'tp'), may hold values from -0.125 to 0.125
- out_weight: bfloat16 [2304, 2304], P('tp'), may hold values from -0.375 to 0.375
- feedforward_gain: float32 [2304], replicated, may hold values from 0.5 to 1.5
- prefill_cache: bfloat16 [8, 2, 1024, 2304], P('seq', None, None, 'tp'), may hold values from -420 to 420
- prefill_offsets: int32 [8], P('seq'), may hold values from 0 to 1024, as said below
- decode_cache: bfloat16 [64, 2, 256, 2304], P('seq', None, None, 'tp'), may hold values from -420 to 420
- decode_lengths: int32 [64], P('seq'), may hold values from 1 to 256, as said below
- request_slot: int32 [64], replicated, may hold values from 0 to 63, each once
Outputs:
- prefill_hidden: bfloat16 [4096, 2304], P('seq')
- decode_hidden: bfloat16 [64, 2304], P('seq')
- prefill_normed: bfloat16 [4096, 2304], P('seq')
- decode_normed: bfloat16 [64, 2304], P('seq')
The draws below stay inside these ranges and needn't reach their ends.
Inputs may be any that keep to these rules, and one draw needn't show every extreme that they name: `request_slot`: each slot is named by exactly one request. `decode_lengths`: some slot holds exactly 256 positions. `prefill_offsets`: some request has exactly 1024 cached positions.
All inputs are finite; a program needn't handle non-finite values.
Results may differ from the reference program's by a relative error of at most 0.014.
The reference program's roundings to bfloat16 on the way (of `normed_in`, `projected`, `weights` and `attended`) count: a program that leaves them out, or rounds other values in their place, can miss the bound.
Values may be sent and summed in bfloat16 or wider, within the bound.
A program may use at most 128 MiB of HBM per device.

```python
import math
import jax
import jax.numpy as jnp
from jax import lax

D = 2304
HEADS = 36
HEAD = 64
SPAN = 512
CMAX = 256
PMAX = 1024
NDEC = 64
PRE_ROWS = 4096
N_SEQ = 8
N_TP = 4


def kv_values(key, shape):
    return jax.random.truncated_normal(key, -6.0, 6.0, shape, jnp.float32)


def draw_decode_cache(key, part):
    return kv_values(key, (NDEC, 2, CMAX, HEADS * HEAD)).astype(jnp.bfloat16)


def draw_prefill_cache(key, part):
    return kv_values(key, (N_SEQ, 2, PMAX, HEADS * HEAD)).astype(jnp.bfloat16)


def draw_decode_lengths(key, part):
    lengths = jax.random.randint(key, (NDEC,), 1, CMAX + 1, dtype=jnp.int32)
    longest = jax.random.randint(jax.random.fold_in(key, 7), (), 0, NDEC, dtype=jnp.int32)
    return lengths.at[longest].set(CMAX)


def draw_prefill_offsets(key, part):
    offsets = jax.random.randint(key, (N_SEQ,), 0, PMAX + 1, dtype=jnp.int32)
    longest = jax.random.randint(jax.random.fold_in(key, 11), (), 0, N_SEQ, dtype=jnp.int32)
    return offsets.at[longest].set(PMAX)


def levels(rng, dims, shards, low, high):
    level, own = 1.0, jax.random.fold_in(rng, 6)
    for dim, shards_of in shards:
        draws = jnp.exp(jax.random.uniform(jax.random.fold_in(own, dim), (shards_of,), jnp.float32, low / len(shards), high / len(shards)))
        level = level * jnp.repeat(draws, dims[dim] // shards_of).reshape([-1 if axis == dim else 1 for axis in range(len(dims))])
    return level


def bell_draw(own_key, shape, deviation, reach, cuts=(), kind=jnp.bfloat16):
    array = jax.random.normal(own_key, shape, jnp.float32) * deviation
    if len(cuts) > 0:
        array = levels(own_key, shape, cuts, -0.22, 0.18) * array
    return jnp.clip(array, min=-reach, max=reach).astype(kind)


def setup_inputs(seed: int = 0) -> dict:
    keys = jax.random.split(jax.random.key(seed), 12)
    prefill_tokens = bell_draw(keys[0], (PRE_ROWS, D), 1.0, 6.0, ((0, 8),))
    decode_tokens = bell_draw(keys[1], (NDEC, D), 1.0, 6.0, ((0, 8),))
    attention_gain = jnp.clip(1.0 + 0.1 * jax.random.normal(keys[2], (D,), jnp.float32), 0.5, 1.5)
    qkv_weight = bell_draw(keys[3], (D, 3, HEADS * HEAD), D ** -0.5, 0.125, ((2, 4),))
    out_weight = bell_draw(keys[4], (HEADS * HEAD, D), (4 * HEAD) ** -0.5, 0.375, ((0, 4),))
    feedforward_gain = jnp.clip(1.0 + 0.1 * jax.random.normal(keys[5], (D,), jnp.float32), 0.5, 1.5)
    prefill_cache = draw_prefill_cache(jax.random.fold_in(keys[11], 71), 0)
    prefill_offsets = draw_prefill_offsets(jax.random.fold_in(keys[11], 71), 0)
    decode_cache = draw_decode_cache(jax.random.fold_in(keys[11], 71), 0)
    decode_lengths = draw_decode_lengths(jax.random.fold_in(keys[11], 71), 0)
    request_slot = jax.random.permutation(keys[10], NDEC).astype(jnp.int32)
    return {"prefill_tokens": prefill_tokens, "decode_tokens": decode_tokens, "attention_gain": attention_gain, "qkv_weight": qkv_weight, "out_weight": out_weight, "feedforward_gain": feedforward_gain, "prefill_cache": prefill_cache, "prefill_offsets": prefill_offsets, "decode_cache": decode_cache, "decode_lengths": decode_lengths, "request_slot": request_slot}


RMS_EPSILON = 1e-05
ROPE_BASE = 10000.0
NEGATIVE = -1e+30

def rms_norm(stream, gain):
    widened = stream.astype(jnp.float32)
    inverse = lax.rsqrt(lax.optimization_barrier(jnp.mean(widened * widened, axis=-1, keepdims=True)) + RMS_EPSILON)
    return widened * inverse * gain

def rotate(vectors, positions):
    half_dim = vectors.shape[-1] // 2
    exponent = jnp.arange(half_dim, dtype=jnp.float32) * (2.0 / vectors.shape[-1])
    frequency = ROPE_BASE ** (-exponent)
    angles = positions[:, None] * frequency[None, :]
    cosine = jnp.cos(angles)[:, None, :]
    sine_part = jnp.sin(angles)[:, None, :]
    first_half = vectors[..., :half_dim]
    second_half = vectors[..., half_dim:]
    return jnp.concatenate([first_half * cosine - second_half * sine_part, second_half * cosine + first_half * sine_part], axis=-1)

def softmax_mix(scores, visible, values_all):
    scores = jnp.where(visible, scores, NEGATIVE)
    row_peak = lax.optimization_barrier(jnp.max(scores, axis=-1, keepdims=True))
    exps = jnp.exp(scores - row_peak)
    weights = (exps / lax.optimization_barrier(jnp.sum(exps, axis=-1, keepdims=True))).astype(jnp.bfloat16)
    return jnp.einsum('hqk,khe->qhe', weights.astype(jnp.float32), values_all.astype(jnp.float32))

def reference(prefill_tokens, decode_tokens, attention_gain, qkv_weight, out_weight, feedforward_gain, prefill_cache, prefill_offsets, decode_cache, decode_lengths, request_slot):
    score_scale = 1.0 / math.sqrt(HEAD)
    tokens_all = jnp.concatenate([prefill_tokens, decode_tokens], axis=0)
    normed_in = rms_norm(tokens_all, attention_gain).astype(jnp.bfloat16)
    projected = jnp.dot(normed_in, qkv_weight.reshape(D, 3 * HEADS * HEAD), preferred_element_type=jnp.float32).astype(jnp.bfloat16)
    projected = projected.reshape(-1, 3, HEADS, HEAD)
    prefill_part = projected[:N_SEQ * SPAN].reshape(N_SEQ, SPAN, 3, HEADS, HEAD)
    decode_part = projected[N_SEQ * SPAN:]

    def prefill_one(inputs):
        block_rows, cache_pair, offset = inputs
        positions = offset.astype(jnp.float32) + jnp.arange(SPAN, dtype=jnp.float32)
        queries = rotate(block_rows[:, 0].astype(jnp.float32), positions).astype(jnp.bfloat16)
        new_keys = rotate(block_rows[:, 1].astype(jnp.float32), positions).astype(jnp.bfloat16)
        keys_all = jnp.concatenate([cache_pair[0].reshape(PMAX, HEADS, HEAD), new_keys], axis=0)
        values_all = jnp.concatenate([cache_pair[1].reshape(PMAX, HEADS, HEAD), block_rows[:, 2]], axis=0)
        scores = jnp.einsum('qhe,khe->hqk', queries.astype(jnp.float32), keys_all.astype(jnp.float32)) * score_scale
        cache_visible = jnp.arange(PMAX, dtype=jnp.int32) < offset
        causal = jnp.arange(SPAN, dtype=jnp.int32)[None, :] <= jnp.arange(SPAN, dtype=jnp.int32)[:, None]
        visible = jnp.concatenate([jnp.broadcast_to(cache_visible[None, :], (SPAN, PMAX)), causal], axis=1)
        attended = softmax_mix(scores, visible[None], values_all)
        return attended.reshape(SPAN, HEADS * HEAD).astype(jnp.bfloat16)
    prefill_out = lax.map(prefill_one, (prefill_part, prefill_cache, prefill_offsets)).reshape(N_SEQ * SPAN, HEADS * HEAD)

    def decode_one(inputs):
        block_rows, slot_index = inputs
        cache_pair = decode_cache[slot_index]
        length = decode_lengths[slot_index]
        positions = length.astype(jnp.float32).reshape(1)
        queries = rotate(block_rows[None, 0].astype(jnp.float32), positions).astype(jnp.bfloat16)
        new_keys = rotate(block_rows[None, 1].astype(jnp.float32), positions).astype(jnp.bfloat16)
        keys_all = jnp.concatenate([cache_pair[0].reshape(CMAX, HEADS, HEAD), new_keys], axis=0)
        values_all = jnp.concatenate([cache_pair[1].reshape(CMAX, HEADS, HEAD), block_rows[None, 2]], axis=0)
        scores = jnp.einsum('qhe,khe->hqk', queries.astype(jnp.float32), keys_all.astype(jnp.float32)) * score_scale
        visible = jnp.concatenate([jnp.arange(CMAX, dtype=jnp.int32) < length, jnp.ones((1,), dtype=bool)])
        attended = softmax_mix(scores, visible[None, None, :], values_all)
        return attended.reshape(HEADS * HEAD).astype(jnp.bfloat16)
    decode_out = lax.map(decode_one, (decode_part, request_slot))
    attended_all = jnp.concatenate([prefill_out, decode_out], axis=0)
    group_width = HEADS * HEAD // N_TP
    combined = jnp.zeros((attended_all.shape[0], D), jnp.float32)
    for group_index in range(N_TP):
        low = group_index * group_width
        partial_value = jnp.dot(attended_all[:, low:low + group_width], out_weight[low:low + group_width], preferred_element_type=jnp.float32).astype(jnp.bfloat16)
        partial_value = lax.optimization_barrier(partial_value)
        combined = combined + partial_value.astype(jnp.float32)
    hidden = (tokens_all.astype(jnp.float32) + combined).astype(jnp.bfloat16)
    normed = rms_norm(hidden, feedforward_gain).astype(jnp.bfloat16)
    split_row = N_SEQ * SPAN
    return (hidden[:split_row], hidden[split_row:], normed[:split_row], normed[split_row:])
```

```python
import functools

import jax
import jax.numpy as jnp
import numpy as np
from jax import lax
from jax.experimental import pallas as pl
from jax.experimental.pallas import tpu as pltpu
from jax.sharding import PartitionSpec as P

HEAD = 64
HALF = HEAD // 2
RMS_EPSILON = 1e-05
ROPE_BASE = 10000.0
NEGATIVE = -1e30
GROUP = 3
PIECE = 64
FREQUENCY = [float(np.float32(ROPE_BASE ** (-2.0 * i / HEAD))) for i in range(HALF)]
MIB = 1 << 20
F32, BF16 = jnp.float32, jnp.bfloat16
MESH = pl.DeviceIdType.MESH
VMEM = pltpu.VMEM
VSPEC = pl.BlockSpec(memory_space=pltpu.VMEM)
HSPEC = pl.BlockSpec(memory_space=pltpu.HBM)
SSPEC = pl.BlockSpec(memory_space=pltpu.SMEM)


def dot(a, b, ca, cb):
    return lax.dot_general(a, b, (((ca,), (cb,)), ((), ())), preferred_element_type=F32)


def rms_rows(x, gain):
    inverse = lax.rsqrt(jnp.mean(x * x, axis=-1, keepdims=True) + RMS_EPSILON)
    return (x * inverse * gain).astype(BF16)


def rotate_columns(x, cosine, sine, scale):
    pieces = []
    for head in range(x.shape[0] // HEAD):
        a = x[head * HEAD : head * HEAD + HALF]
        b = x[head * HEAD + HALF : (head + 1) * HEAD]
        pieces.append(a * cosine - b * sine)
        pieces.append(b * cosine + a * sine)
    turned = jnp.concatenate(pieces, axis=0).astype(BF16)
    return turned if scale is None else (turned.astype(F32) * scale).astype(BF16)


def block_kernel(
    n, chunks, tok_hbm, wqkv_hbm, wo_hbm, pcache_hbm, dcache_hbm, dtok_hbm, gain_hbm, gain2_hbm,
    length_hbm, slot_hbm, offset_ref,
    hid_ref, dhid_ref, nor_ref, dnor_ref,
    tok, wqkv, wo, pcache, dcache, dtok, gain, gain2, lengths, slot,
    normed, proj, arrived, results, routed, part, got1, pair, got2, dpart, dgot1, dpair, dgot2, dhalf,
    load_sem, send1, recv1, send2, recv2, s1, r1, s2, r2, s3, r3,
):
    rows, width = tok.shape
    slots = dhid_ref.shape[0]
    local = wo.shape[0]
    heads = local // HEAD
    wide = GROUP * HEAD
    pieces = rows // PIECE
    own_rows = PIECE // 2
    half_width = width // 2
    keys = pcache.shape[2]
    dkeys = dcache.shape[3]
    half = rows // 2
    seq = lax.axis_index("seq")
    tp = lax.axis_index("tp")
    side = lax.rem(tp, 2)
    core = tp + 1 - 2 * side
    across = lax.rem(tp + 2, 4)
    mine = pl.multiple_of(side * own_rows, own_rows)
    other = pl.multiple_of((1 - side) * own_rows, own_rows)

    pairs = (
        (length_hbm, lengths),
        (gain_hbm, gain),
        (dtok_hbm, dtok),
        (gain2_hbm, gain2),
        (slot_hbm, slot),
        (tok_hbm.at[:half], tok.at[:half]),
        (wqkv_hbm.at[0], wqkv.at[0]),
        (wqkv_hbm.at[1], wqkv.at[1]),
        (wqkv_hbm.at[2], wqkv.at[2]),
        (pcache_hbm.at[0], pcache.at[0]),
        (pcache_hbm.at[1], pcache.at[1]),
        (wo_hbm, wo),
        (tok_hbm.at[half:], tok.at[half:]),
        (dcache_hbm, dcache),
    )
    loads = [pltpu.make_async_copy(src, dst, load_sem.at[i]) for i, (src, dst) in enumerate(pairs)]
    smalls, loads = loads[:5], loads[5:]
    for load in smalls[:2] + loads[:7] + smalls[2:]:
        load.start()

    barrier = pltpu.get_barrier_semaphore()
    for step in range(1, n):
        pl.semaphore_signal(barrier, inc=1, device_id={"seq": lax.rem(seq + step, n)}, device_id_type=MESH)
    for step in range(1, 4):
        pl.semaphore_signal(barrier, inc=1, device_id={"tp": lax.rem(tp + step, 4)}, device_id_type=MESH)

    def spread(buffer, send, recv):
        return [
            pltpu.make_async_remote_copy(
                src_ref=buffer.at[seq],
                dst_ref=buffer.at[seq],
                send_sem=send.at[step],
                recv_sem=recv.at[step],
                device_id={"seq": lax.rem(seq + step, n)},
                device_id_type=MESH,
            )
            for step in range(1, n)
        ]

    def send(src, dst, ssem, rsem, to):
        return pltpu.make_async_remote_copy(
            src_ref=src, dst_ref=dst, send_sem=ssem, recv_sem=rsem,
            device_id={"tp": to}, device_id_type=MESH,
        )

    def owned(c):
        return pl.ds(c * PIECE + mine, own_rows)

    def others(c):
        return pl.ds(c * PIECE + other, own_rows)

    there = spread(arrived, send1, recv1)
    back = spread(results, send2, recv2)
    first = [
        send(part.at[c, pl.ds(other, own_rows)], got1.at[c], s1.at[c], r1.at[c], core) for c in range(pieces)
    ] + [send(dpart.at[1 - side], dgot1, s1.at[pieces], r1.at[pieces], core)]
    second = [send(pair.at[c], got2.at[c], s2.at[c], r2.at[c], across) for c in range(pieces)] + [
        send(dpair, dgot2, s2.at[pieces], r2.at[pieces], across)
    ]
    third = [send(hid_ref.at[owned(c)], hid_ref.at[owned(c)], s3.at[c], r3.at[c], core) for c in range(pieces)] + [
        send(dhalf.at[side], dhalf.at[side], s3.at[pieces], r3.at[pieces], core)
    ]

    row = lax.broadcasted_iota(jnp.int32, (HALF, 1), 0)
    frequency = jnp.zeros((HALF, 1), F32)
    for i, value in enumerate(FREQUENCY):
        frequency = jnp.where(row == i, value, frequency)
    angles = frequency * (offset_ref[0].astype(F32) + lax.broadcasted_iota(jnp.int32, (1, rows), 1).astype(F32))
    cosine, sine = jnp.cos(angles), jnp.sin(angles)
    bias = jnp.where(lax.broadcasted_iota(jnp.int32, (1, keys), 1) < offset_ref[0], 0.0, NEGATIVE)
    smalls[0].wait()
    length = lengths[...].reshape(1, slots).astype(F32)
    dangles = frequency * length
    dcos, dsin = jnp.cos(dangles), jnp.sin(dangles)

    smalls[1].wait()
    scale1 = gain[...].reshape(1, width)

    def norm_rows(start, stop):
        for low in range(start, stop, 64):
            normed[low - start : low - start + 64, :] = rms_rows(tok[low : low + 64, :].astype(F32), scale1)

    def project(index, start, stop):
        product = dot(wqkv[index], normed[...], 1, 1).astype(BF16)
        if index < 2:
            product = rotate_columns(
                product.astype(F32), cosine[:, start:stop], sine[:, start:stop], 0.125 if index == 0 else None
            )
        proj[index, :, start:stop] = product

    def attend(start, stop):
        chunk = stop - start
        causal = lax.broadcasted_iota(jnp.int32, (GROUP * chunk, chunk), 1) <= lax.rem(
            lax.broadcasted_iota(jnp.int32, (GROUP * chunk, chunk), 0), chunk
        )
        block = lax.broadcasted_iota(jnp.int32, (chunk, wide), 1) // HEAD
        out = None
        for group in range(heads // GROUP):
            span = slice(group * wide, (group + 1) * wide)
            turned = proj[0, span, start:stop].astype(F32).T
            query = jnp.concatenate(
                [jnp.where(block == i, turned, 0.0).astype(BF16) for i in range(GROUP)], axis=0
            )
            scores = [dot(query, pcache[0, span, :], 1, 0) + bias]
            scores.append(jnp.where(causal, dot(query, proj[1, span, start:stop], 1, 0), NEGATIVE))
            values = [pcache[1, span, :], proj[2, span, start:stop]]
            if start > 0:
                scores.append(dot(query, proj[1, span, :start], 1, 0))
                values.append(proj[2, span, :start])
            peak = functools.reduce(jnp.maximum, [jnp.max(x, axis=-1, keepdims=True) for x in scores])
            exps = [jnp.exp(x - peak) for x in scores]
            total = functools.reduce(jnp.add, [jnp.sum(x, axis=-1, keepdims=True) for x in exps])
            mixed = functools.reduce(
                jnp.add, [dot(x.astype(BF16), v, 1, 1) for x, v in zip(exps, values)]
            ) * (1.0 / total)
            own = mixed[:chunk]
            for i in range(1, GROUP):
                own = jnp.where(block == i, mixed[i * chunk : (i + 1) * chunk], own)
            term = dot(own.astype(BF16), wo[span, :], 1, 0)
            out = term if out is None else out + term
        out = out.astype(BF16)
        for low in range(start, stop, PIECE):
            c = low // PIECE
            part[c] = out[low - start : low - start + PIECE]
            first[c].start()

    def cross(c):
        first[c].wait_recv()
        if c < pieces:
            pair[c] = (part[c, pl.ds(mine, own_rows)].astype(F32) + got1[c].astype(F32)).astype(BF16)
        else:
            dpair[...] = (dpart[side].astype(F32) + dgot1[...].astype(F32)).astype(BF16)
        second[c].start()

    def finish(c):
        second[c].wait_recv()
        if c < pieces:
            combined = pair[c].astype(F32) + got2[c].astype(F32)
            hidden = (tok[owned(c), :].astype(F32) + combined).astype(BF16)
            hid_ref[owned(c), :] = hidden
            third[c].start()
            nor_ref[owned(c), :] = rms_rows(hidden.astype(F32), scale2)
        else:
            combined = dpair[...].astype(F32) + dgot2[...].astype(F32)
            tokens = jnp.where(side == 0, dtok[:, :half_width].astype(F32), dtok[:, half_width:].astype(F32))
            dhalf[side] = (tokens + combined).astype(BF16)
            third[c].start()

    def settle(c):
        third[c].wait_recv()
        if c < pieces:
            nor_ref[others(c), :] = rms_rows(hid_ref[others(c), :].astype(F32), scale2)
        else:
            hidden = jnp.concatenate([dhalf[0], dhalf[1]], axis=1)
            dhid_ref[...] = hidden
            dnor_ref[...] = rms_rows(hidden.astype(F32), scale2)

    loads[0].wait()
    norm_rows(0, half)
    for index in range(3):
        loads[1 + index].wait()
        project(index, 0, half)
    for load in loads[7:]:
        load.start()
    for load in loads[4:7]:
        load.wait()
    pl.semaphore_wait(barrier, n + 2)
    attend(*chunks[0])

    for load in smalls[2:]:
        load.wait()
    scale2 = gain2[...].reshape(1, width)
    dnormed = rms_rows(dtok[...].astype(F32), scale1)
    for index in range(3):
        arrived[seq, index] = dot(dnormed, wqkv[index], 1, 1).astype(BF16)
    for copy in there:
        copy.start()
    cross(0)
    attend(*chunks[1])
    loads[7].wait()
    norm_rows(half, rows)
    cross(1)
    attend(*chunks[2])
    project(0, half, rows)
    cross(2)
    project(1, half, rows)
    cross(3)
    project(2, half, rows)
    attend(*chunks[3])
    finish(0)
    finish(1)
    cross(4)
    cross(5)
    settle(0)
    settle(1)

    for copy in there:
        copy.wait()
    total = n * slots
    chosen = seq * slots + lax.broadcasted_iota(jnp.int32, (slots, total), 0)
    slot_row = slot[...].reshape(1, total)
    pick = (slot_row == chosen).astype(F32).astype(BF16)
    placing = (slot_row == lax.broadcasted_iota(jnp.int32, (total, total), 0)).astype(F32).astype(BF16)

    def gathered(which):
        return arrived[:, which].astype(F32).reshape(total, local).astype(BF16)

    q = rotate_columns(dot(gathered(0), pick, 0, 1).astype(BF16).astype(F32), dcos, dsin, 0.125).astype(F32)
    k = rotate_columns(dot(gathered(1), pick, 0, 1).astype(BF16).astype(F32), dcos, dsin, None).astype(F32)
    v = dot(pick, gathered(2), 1, 0).astype(BF16).astype(F32)
    padded = 16
    own_head = (
        lax.broadcasted_iota(jnp.int32, (local, padded), 0) // HEAD
        == lax.broadcasted_iota(jnp.int32, (local, padded), 1)
    )
    own_lane = (
        lax.broadcasted_iota(jnp.int32, (padded, local), 1) // HEAD
        == lax.broadcasted_iota(jnp.int32, (padded, local), 0)
    )
    loads[8].wait()
    position = lax.broadcasted_iota(jnp.int32, (1, dkeys), 1).astype(F32)
    product = q * k
    own = jnp.concatenate(
        [
            jnp.sum(product[head * HEAD : (head + 1) * HEAD], axis=0, keepdims=True)
            if head < heads
            else jnp.zeros((1, slots), F32)
            for head in range(padded)
        ],
        axis=0,
    )
    own = jnp.concatenate([own[:, s : s + 1] for s in range(slots)], axis=0)
    scores = []
    for s in range(slots):
        query = jnp.where(own_head, q[:, s : s + 1], 0.0).astype(BF16)
        hidden_keys = jnp.where(position < length[:, s : s + 1], 0.0, NEGATIVE)
        scores.append(dot(query, dcache[s, 0], 0, 0) + hidden_keys)
    scores = jnp.concatenate(scores, axis=0)
    peak = jnp.maximum(jnp.max(scores, axis=-1, keepdims=True), own)
    exps = jnp.exp(scores - peak)
    own_exp = jnp.exp(own - peak)
    denominator = jnp.sum(exps, axis=-1, keepdims=True) + own_exp
    weights = (exps / denominator).astype(BF16)
    own_weight = (own_exp / denominator).astype(BF16).astype(F32)
    attended = []
    for s in range(slots):
        span = slice(s * padded, (s + 1) * padded)
        mixed = dot(weights[span], dcache[s, 1], 1, 1) + own_weight[span] * v[s : s + 1]
        attended.append(jnp.sum(jnp.where(own_lane, mixed, 0.0), axis=0, keepdims=True))
    results[seq] = jnp.concatenate(attended, axis=0).astype(BF16)
    for copy in back:
        copy.start()

    attend(*chunks[4])
    finish(2)
    finish(3)
    cross(6)
    cross(7)
    settle(2)
    settle(3)
    for copy in back:
        copy.wait()
    every = results[...].astype(F32).reshape(total, local).astype(BF16)
    routed[...] = dot(placing, every, 0, 0)
    returned = routed[pl.ds(pl.multiple_of(seq * slots, slots), slots), :].astype(BF16)
    mixed = dot(returned, wo[...], 1, 0).astype(BF16)
    dpart[0] = mixed[:, :half_width]
    dpart[1] = mixed[:, half_width:]
    first[pieces].start()
    finish(4)
    cross(pieces)
    finish(5)
    settle(4)
    settle(5)
    finish(6)
    settle(6)
    finish(7)
    finish(pieces)
    settle(7)
    settle(pieces)
    for copy in first + second + third:
        copy.wait_send()


def block(n, tokens, wqkv, wo, pcache, dcache, dtokens, gain, gain2, lengths, slot, offset):
    rows, width = tokens.shape
    slots = dtokens.shape[0]
    local = wo.shape[0]
    pieces = rows // PIECE
    chunks = ((0, 64), (64, 128), (128, 256), (256, 384), (384, 512))
    buffer = VMEM((pieces, PIECE // 2, width), BF16)
    dbuffer = VMEM((slots, width // 2), BF16)
    dhalves = VMEM((2, slots, width // 2), BF16)
    sem = pltpu.SemaphoreType.DMA((pieces + 1,))
    args = (tokens, wqkv, wo, pcache, dcache, dtokens, gain, gain2, lengths, slot)
    args = [pltpu.with_memory_space_constraint(x, pltpu.HBM) for x in args]
    return pl.pallas_call(
        functools.partial(block_kernel, n, chunks),
        in_specs=[HSPEC] * 10 + [SSPEC],
        out_specs=[VSPEC] * 4,
        out_shape=[jax.ShapeDtypeStruct((x, width), BF16) for x in (rows, slots, rows, slots)],
        scratch_shapes=[VMEM(x.shape, x.dtype) for x in args]
        + [
            VMEM((rows // 2, width), BF16),
            VMEM((3, local, rows), BF16),
            VMEM((n, 3, slots, local), BF16),
            VMEM((n, slots, local), BF16),
            VMEM((n * slots, local), F32),
            VMEM((pieces, PIECE, width), BF16),
            buffer, buffer, buffer,
            dhalves, dbuffer, dbuffer, dbuffer, dhalves,
            pltpu.SemaphoreType.DMA((14,)),
        ]
        + [pltpu.SemaphoreType.DMA((n,))] * 4
        + [sem] * 6,
        compiler_params=pltpu.CompilerParams(
            collective_id=0, has_side_effects=True, vmem_limit_bytes=44 * MIB
        ),
        name="block",
    )(*args, offset)


def deliver_kernel(hid, dhid, nor, dnor, hid_out, dhid_out, nor_out, dnor_out, sem):
    rows = hid.shape[0]
    step = rows // 4
    copies = []
    for src, dst in ((hid, hid_out), (nor, nor_out)):
        for i in range(4):
            span = pl.ds(i * step, step)
            copies.append((src.at[span], dst.at[span]))
    copies += [(dhid, dhid_out), (dnor, dnor_out)]
    copies = [pltpu.make_async_copy(src, dst, sem.at[i]) for i, (src, dst) in enumerate(copies)]
    for copy in copies:
        copy.start()
    for copy in copies:
        copy.wait()


def deliver(*arrays):
    return pl.pallas_call(
        deliver_kernel,
        in_specs=[VSPEC] * 4,
        out_specs=[HSPEC] * 4,
        out_shape=[jax.ShapeDtypeStruct(x.shape, BF16) for x in arrays],
        scratch_shapes=[pltpu.SemaphoreType.DMA((10,))],
        compiler_params=pltpu.CompilerParams(vmem_limit_bytes=16 * MIB),
        name="deliver",
    )(*arrays)


def local_step(
    n,
    prefill_tokens,
    decode_tokens,
    attention_gain,
    qkv_weight,
    out_weight,
    feedforward_gain,
    prefill_cache,
    prefill_offsets,
    decode_cache,
    decode_lengths,
    request_slot,
):
    hidden, dhidden, normed, dnormed = block(
        n, prefill_tokens, qkv_weight.transpose(1, 2, 0), out_weight, prefill_cache[0].transpose(0, 2, 1),
        decode_cache.transpose(0, 1, 3, 2), decode_tokens, attention_gain, feedforward_gain, decode_lengths,
        request_slot, prefill_offsets,
    )
    hidden, dhidden, normed, dnormed = deliver(hidden, dhidden, normed, dnormed)
    return hidden, dhidden, normed, dnormed


def solution(mesh):
    placed = (
        P("seq", None),
        P("seq", None),
        P(),
        P(None, None, "tp"),
        P("tp", None),
        P(),
        P("seq", None, None, "tp"),
        P("seq"),
        P("seq", None, None, "tp"),
        P("seq"),
        P(),
    )
    return jax.shard_map(
        functools.partial(local_step, mesh.shape["seq"]),
        mesh=mesh,
        in_specs=placed,
        out_specs=(P("seq", None), P("seq", None), P("seq", None), P("seq", None)),
        check_vma=False,
    )
```

```python
import functools

import jax
import jax.numpy as jnp
import numpy as np
from jax import lax
from jax.experimental import pallas as pl
from jax.experimental.pallas import tpu as pltpu
from jax.sharding import PartitionSpec as P

HEAD = 64
HALF = HEAD // 2
RMS_EPSILON = 1e-05
ROPE_BASE = 10000.0
NEGATIVE = -1e30
GROUP = 3
PIECE = 64
FREQUENCY = [float(np.float32(ROPE_BASE ** (-2.0 * i / HEAD))) for i in range(HALF)]
MIB = 1 << 20
F32, BF16 = jnp.float32, jnp.bfloat16
MESH = pl.DeviceIdType.MESH
VMEM = pltpu.VMEM
VSPEC = pl.BlockSpec(memory_space=pltpu.VMEM)
HSPEC = pl.BlockSpec(memory_space=pltpu.HBM)
SSPEC = pl.BlockSpec(memory_space=pltpu.SMEM)


def dot(a, b, ca, cb):
    return lax.dot_general(a, b, (((ca,), (cb,)), ((), ())), preferred_element_type=F32)


def rms_rows(x, gain):
    inverse = lax.rsqrt(jnp.mean(x * x, axis=-1, keepdims=True) + RMS_EPSILON)
    return (x * inverse * gain).astype(BF16)


def rotate_columns(x, cosine, sine, scale):
    pieces = []
    for head in range(x.shape[0] // HEAD):
        a = x[head * HEAD : head * HEAD + HALF]
        b = x[head * HEAD + HALF : (head + 1) * HEAD]
        pieces.append(a * cosine - b * sine)
        pieces.append(b * cosine + a * sine)
    turned = jnp.concatenate(pieces, axis=0).astype(BF16)
    return turned if scale is None else (turned.astype(F32) * scale).astype(BF16)


def block_kernel(
    n, chunks, tok_hbm, wqkv_hbm, wo_hbm, pcache_hbm, dcache_hbm, dtok_hbm, gain_hbm, gain2_hbm,
    length_hbm, slot_hbm, offset_ref,
    hid_ref, dhid_ref, nor_ref, dnor_ref,
    tok, wqkv, wo, pcache, dcache, dtok, gain, gain2, lengths, slot,
    normed, proj, arrived, results, routed, part, got1, pair, got2, dpart, dgot1, dpair, dgot2, dhalf,
    load_sem, send1, recv1, send2, recv2, s1, r1, s2, r2, s3, r3,
):
    rows, width = tok.shape
    slots = dhid_ref.shape[0]
    local = wo.shape[0]
    heads = local // HEAD
    wide = GROUP * HEAD
    pieces = rows // PIECE
    own_rows = PIECE // 2
    half_width = width // 2
    keys = pcache.shape[2]
    dkeys = dcache.shape[3]
    half = rows // 2
    seq = lax.axis_index("seq")
    tp = lax.axis_index("tp")
    side = lax.rem(tp, 2)
    core = tp + 1 - 2 * side
    across = lax.rem(tp + 2, 4)
    mine = pl.multiple_of(side * own_rows, own_rows)
    other = pl.multiple_of((1 - side) * own_rows, own_rows)

    pairs = (
        (length_hbm, lengths),
        (gain_hbm, gain),
        (dtok_hbm, dtok),
        (gain2_hbm, gain2),
        (slot_hbm, slot),
        (tok_hbm.at[:half], tok.at[:half]),
        (wqkv_hbm.at[0], wqkv.at[0]),
        (wqkv_hbm.at[1], wqkv.at[1]),
        (wqkv_hbm.at[2], wqkv.at[2]),
        (pcache_hbm.at[0], pcache.at[0]),
        (pcache_hbm.at[1], pcache.at[1]),
        (wo_hbm, wo),
        (tok_hbm.at[half:], tok.at[half:]),
        (dcache_hbm, dcache),
    )
    loads = [pltpu.make_async_copy(src, dst, load_sem.at[i]) for i, (src, dst) in enumerate(pairs)]
    smalls, loads = loads[:5], loads[5:]
    for load in smalls[:2] + loads[:4]:
        load.start()

    barrier = pltpu.get_barrier_semaphore()
    for step in range(1, n):
        pl.semaphore_signal(barrier, inc=1, device_id={"seq": lax.rem(seq + step, n)}, device_id_type=MESH)
    for step in range(1, 4):
        pl.semaphore_signal(barrier, inc=1, device_id={"tp": lax.rem(tp + step, 4)}, device_id_type=MESH)

    def spread(buffer, send, recv):
        return [
            pltpu.make_async_remote_copy(
                src_ref=buffer.at[seq],
                dst_ref=buffer.at[seq],
                send_sem=send.at[step],
                recv_sem=recv.at[step],
                device_id={"seq": lax.rem(seq + step, n)},
                device_id_type=MESH,
            )
            for step in range(1, n)
        ]

    def send(src, dst, ssem, rsem, to):
        return pltpu.make_async_remote_copy(
            src_ref=src, dst_ref=dst, send_sem=ssem, recv_sem=rsem,
            device_id={"tp": to}, device_id_type=MESH,
        )

    def owned(c):
        return pl.ds(c * PIECE + mine, own_rows)

    def others(c):
        return pl.ds(c * PIECE + other, own_rows)

    there = spread(arrived, send1, recv1)
    back = spread(results, send2, recv2)
    first = [
        send(part.at[c, pl.ds(other, own_rows)], got1.at[c], s1.at[c], r1.at[c], core) for c in range(pieces)
    ] + [send(dpart.at[1 - side], dgot1, s1.at[pieces], r1.at[pieces], core)]
    second = [send(pair.at[c], got2.at[c], s2.at[c], r2.at[c], across) for c in range(pieces)] + [
        send(dpair, dgot2, s2.at[pieces], r2.at[pieces], across)
    ]
    third = [send(hid_ref.at[owned(c)], hid_ref.at[owned(c)], s3.at[c], r3.at[c], core) for c in range(pieces)] + [
        send(dhalf.at[side], dhalf.at[side], s3.at[pieces], r3.at[pieces], core)
    ]

    row = lax.broadcasted_iota(jnp.int32, (HALF, 1), 0)
    frequency = jnp.zeros((HALF, 1), F32)
    for i, value in enumerate(FREQUENCY):
        frequency = jnp.where(row == i, value, frequency)
    angles = frequency * (offset_ref[0].astype(F32) + lax.broadcasted_iota(jnp.int32, (1, rows), 1).astype(F32))
    cosine, sine = jnp.cos(angles), jnp.sin(angles)
    bias = jnp.where(lax.broadcasted_iota(jnp.int32, (1, keys), 1) < offset_ref[0], 0.0, NEGATIVE)
    smalls[0].wait()
    length = lengths[...].reshape(1, slots).astype(F32)
    dangles = frequency * length
    dcos, dsin = jnp.cos(dangles), jnp.sin(dangles)

    smalls[1].wait()
    scale1 = gain[...].reshape(1, width)

    def norm_rows(start, stop):
        for low in range(start, stop, 64):
            normed[low - start : low - start + 64, :] = rms_rows(tok[low : low + 64, :].astype(F32), scale1)

    def project(index, start, stop):
        product = dot(wqkv[index], normed[...], 1, 1).astype(BF16)
        if index < 2:
            product = rotate_columns(
                product.astype(F32), cosine[:, start:stop], sine[:, start:stop], 0.125 if index == 0 else None
            )
        proj[index, :, start:stop] = product

    def attend(start, stop):
        chunk = stop - start
        causal = lax.broadcasted_iota(jnp.int32, (GROUP * chunk, chunk), 1) <= lax.rem(
            lax.broadcasted_iota(jnp.int32, (GROUP * chunk, chunk), 0), chunk
        )
        block = lax.broadcasted_iota(jnp.int32, (chunk, wide), 1) // HEAD
        mixes = []
        for group in range(heads // GROUP):
            span = slice(group * wide, (group + 1) * wide)
            turned = proj[0, span, start:stop].astype(F32).T
            query = jnp.concatenate(
                [jnp.where(block == i, turned, 0.0).astype(BF16) for i in range(GROUP)], axis=0
            )
            scores = [dot(query, pcache[0, span, :], 1, 0) + bias]
            scores.append(jnp.where(causal, dot(query, proj[1, span, start:stop], 1, 0), NEGATIVE))
            values = [pcache[1, span, :], proj[2, span, start:stop]]
            if start > 0:
                scores.append(dot(query, proj[1, span, :start], 1, 0))
                values.append(proj[2, span, :start])
            peak = functools.reduce(jnp.maximum, [jnp.max(x, axis=-1, keepdims=True) for x in scores])
            exps = [jnp.exp(x - peak) for x in scores]
            total = functools.reduce(jnp.add, [jnp.sum(x, axis=-1, keepdims=True) for x in exps])
            mixed = functools.reduce(
                jnp.add, [dot(x.astype(BF16), v, 1, 1) for x, v in zip(exps, values)]
            ) * (1.0 / total)
            own = mixed[:chunk]
            for i in range(1, GROUP):
                own = jnp.where(block == i, mixed[i * chunk : (i + 1) * chunk], own)
            mixes.append(own.astype(BF16))
        out = functools.reduce(
            jnp.add, [dot(x, wo[g * wide : (g + 1) * wide, :], 1, 0) for g, x in enumerate(mixes)]
        ).astype(BF16)
        for low in range(start, stop, PIECE):
            c = low // PIECE
            part[c] = out[low - start : low - start + PIECE]

    def launch(*cs):
        for c in cs:
            first[c].start()

    def cross(*cs):
        for c in cs:
            first[c].wait_recv()
        for c in cs:
            if c < pieces:
                pair[c] = (part[c, pl.ds(mine, own_rows)].astype(F32) + got1[c].astype(F32)).astype(BF16)
            else:
                dpair[...] = (dpart[side].astype(F32) + dgot1[...].astype(F32)).astype(BF16)
        for c in cs:
            second[c].start()

    def finish(*cs):
        for c in cs:
            second[c].wait_recv()
        for c in cs:
            if c < pieces:
                combined = pair[c].astype(F32) + got2[c].astype(F32)
                hid_ref[owned(c), :] = (tok[owned(c), :].astype(F32) + combined).astype(BF16)
            else:
                combined = dpair[...].astype(F32) + dgot2[...].astype(F32)
                tokens = jnp.where(
                    side == 0, dtok[:, :half_width].astype(F32), dtok[:, half_width:].astype(F32)
                )
                dhalf[side] = (tokens + combined).astype(BF16)
        for c in cs:
            third[c].start()

    def settle(*cs):
        for c in cs:
            third[c].wait_recv()
        for c in cs:
            if c < pieces:
                span = slice(c * PIECE, (c + 1) * PIECE)
                nor_ref[span, :] = rms_rows(hid_ref[span, :].astype(F32), scale2)
            else:
                hidden = jnp.concatenate([dhalf[0], dhalf[1]], axis=1)
                dhid_ref[...] = hidden
                dnor_ref[...] = rms_rows(hidden.astype(F32), scale2)

    loads[0].wait()
    norm_rows(0, half)
    for load in loads[4:6]:
        load.start()
    loads[1].wait()
    project(0, 0, half)
    for load in loads[6:8] + smalls[2:]:
        load.start()
    loads[2].wait()
    project(1, 0, half)
    loads[8].start()
    loads[3].wait()
    project(2, 0, half)
    for load in loads[4:7]:
        load.wait()
    pl.semaphore_wait(barrier, n + 2)
    attend(*chunks[0])
    launch(0)

    for load in smalls[2:]:
        load.wait()
    scale2 = gain2[...].reshape(1, width)
    dnormed = rms_rows(dtok[...].astype(F32), scale1)
    for index in range(3):
        arrived[seq, index] = dot(dnormed, wqkv[index], 1, 1).astype(BF16)
    for copy in there:
        copy.start()
    cross(0)
    loads[7].wait()
    norm_rows(half, rows)
    project(0, half, rows)
    attend(*chunks[1])
    launch(1)
    project(1, half, rows)
    cross(1)
    project(2, half, rows)
    attend(*chunks[2])
    launch(2, 3)

    for copy in there:
        copy.wait()
    loads[8].wait()
    total = n * slots
    chosen = seq * slots + lax.broadcasted_iota(jnp.int32, (slots, total), 0)
    slot_row = slot[...].reshape(1, total)
    pick = (slot_row == chosen).astype(F32).astype(BF16)
    placing = (slot_row == lax.broadcasted_iota(jnp.int32, (total, total), 0)).astype(F32).astype(BF16)

    def gathered(which):
        return arrived[:, which].astype(F32).reshape(total, local).astype(BF16)

    q = rotate_columns(dot(gathered(0), pick, 0, 1).astype(BF16).astype(F32), dcos, dsin, 0.125).astype(F32)
    k = rotate_columns(dot(gathered(1), pick, 0, 1).astype(BF16).astype(F32), dcos, dsin, None).astype(F32)
    v = dot(pick, gathered(2), 1, 0).astype(BF16).astype(F32)
    cross(2, 3)
    attend(*chunks[3])
    launch(4, 5)
    finish(0, 1)
    cross(4, 5)

    padded = 16
    own_head = (
        lax.broadcasted_iota(jnp.int32, (local, padded), 0) // HEAD
        == lax.broadcasted_iota(jnp.int32, (local, padded), 1)
    )
    own_lane = (
        lax.broadcasted_iota(jnp.int32, (padded, local), 1) // HEAD
        == lax.broadcasted_iota(jnp.int32, (padded, local), 0)
    )
    position = lax.broadcasted_iota(jnp.int32, (1, dkeys), 1).astype(F32)
    product = q * k
    own = jnp.concatenate(
        [
            jnp.sum(product[head * HEAD : (head + 1) * HEAD], axis=0, keepdims=True)
            if head < heads
            else jnp.zeros((1, slots), F32)
            for head in range(padded)
        ],
        axis=0,
    )
    own = jnp.concatenate([own[:, s : s + 1] for s in range(slots)], axis=0)
    scores = []
    for s in range(slots):
        query = jnp.where(own_head, q[:, s : s + 1], 0.0).astype(BF16)
        hidden_keys = jnp.where(position < length[:, s : s + 1], 0.0, NEGATIVE)
        scores.append(dot(query, dcache[s, 0], 0, 0) + hidden_keys)
    scores = jnp.concatenate(scores, axis=0)
    peak = jnp.maximum(jnp.max(scores, axis=-1, keepdims=True), own)
    exps = jnp.exp(scores - peak)
    own_exp = jnp.exp(own - peak)
    denominator = jnp.sum(exps, axis=-1, keepdims=True) + own_exp
    weights = (exps / denominator).astype(BF16)
    own_weight = (own_exp / denominator).astype(BF16).astype(F32)
    attended = []
    for s in range(slots):
        span = slice(s * padded, (s + 1) * padded)
        mixed = dot(weights[span], dcache[s, 1], 1, 1) + own_weight[span] * v[s : s + 1]
        attended.append(jnp.sum(jnp.where(own_lane, mixed, 0.0), axis=0, keepdims=True))
    results[seq] = jnp.concatenate(attended, axis=0).astype(BF16)
    attend(*chunks[4])
    launch(6, 7)
    for copy in back:
        copy.start()
    settle(0, 1)
    finish(2, 3)
    cross(6, 7)
    settle(2, 3)
    for copy in back:
        copy.wait()
    every = results[...].astype(F32).reshape(total, local).astype(BF16)
    routed[...] = dot(placing, every, 0, 0)
    returned = routed[pl.ds(pl.multiple_of(seq * slots, slots), slots), :].astype(BF16)
    mixed = dot(returned, wo[...], 1, 0).astype(BF16)
    dpart[0] = mixed[:, :half_width]
    dpart[1] = mixed[:, half_width:]
    launch(pieces)
    finish(4)
    cross(pieces)
    finish(5)
    settle(4, 5)
    finish(pieces, 6)
    settle(pieces, 6)
    finish(7)
    settle(7)
    for copy in first + second + third:
        copy.wait_send()


def block(n, tokens, wqkv, wo, pcache, dcache, dtokens, gain, gain2, lengths, slot, offset):
    rows, width = tokens.shape
    slots = dtokens.shape[0]
    local = wo.shape[0]
    pieces = rows // PIECE
    chunks = ((0, 64), (64, 128), (128, 256), (256, 384), (384, 512))
    buffer = VMEM((pieces, PIECE // 2, width), BF16)
    dbuffer = VMEM((slots, width // 2), BF16)
    dhalves = VMEM((2, slots, width // 2), BF16)
    sem = pltpu.SemaphoreType.DMA((pieces + 1,))
    args = (tokens, wqkv, wo, pcache, dcache, dtokens, gain, gain2, lengths, slot)
    args = [pltpu.with_memory_space_constraint(x, pltpu.HBM) for x in args]
    return pl.pallas_call(
        functools.partial(block_kernel, n, chunks),
        in_specs=[HSPEC] * 10 + [SSPEC],
        out_specs=[VSPEC] * 4,
        out_shape=[jax.ShapeDtypeStruct((x, width), BF16) for x in (rows, slots, rows, slots)],
        scratch_shapes=[VMEM(x.shape, x.dtype) for x in args]
        + [
            VMEM((rows // 2, width), BF16),
            VMEM((3, local, rows), BF16),
            VMEM((n, 3, slots, local), BF16),
            VMEM((n, slots, local), BF16),
            VMEM((n * slots, local), F32),
            VMEM((pieces, PIECE, width), BF16),
            buffer, buffer, buffer,
            dhalves, dbuffer, dbuffer, dbuffer, dhalves,
            pltpu.SemaphoreType.DMA((14,)),
        ]
        + [pltpu.SemaphoreType.DMA((n,))] * 4
        + [sem] * 6,
        compiler_params=pltpu.CompilerParams(
            collective_id=0, has_side_effects=True, vmem_limit_bytes=44 * MIB
        ),
        name="block",
    )(*args, offset)


def deliver_kernel(hid, dhid, nor, dnor, hid_out, dhid_out, nor_out, dnor_out, sem):
    rows = hid.shape[0]
    step = rows // 4
    copies = []
    for src, dst in ((hid, hid_out), (nor, nor_out)):
        for i in range(4):
            span = pl.ds(i * step, step)
            copies.append((src.at[span], dst.at[span]))
    copies += [(dhid, dhid_out), (dnor, dnor_out)]
    copies = [pltpu.make_async_copy(src, dst, sem.at[i]) for i, (src, dst) in enumerate(copies)]
    for copy in copies:
        copy.start()
    for copy in copies:
        copy.wait()


def deliver(*arrays):
    return pl.pallas_call(
        deliver_kernel,
        in_specs=[VSPEC] * 4,
        out_specs=[HSPEC] * 4,
        out_shape=[jax.ShapeDtypeStruct(x.shape, BF16) for x in arrays],
        scratch_shapes=[pltpu.SemaphoreType.DMA((10,))],
        compiler_params=pltpu.CompilerParams(vmem_limit_bytes=16 * MIB),
        name="deliver",
    )(*arrays)


def local_step(
    n,
    prefill_tokens,
    decode_tokens,
    attention_gain,
    qkv_weight,
    out_weight,
    feedforward_gain,
    prefill_cache,
    prefill_offsets,
    decode_cache,
    decode_lengths,
    request_slot,
):
    hidden, dhidden, normed, dnormed = block(
        n, prefill_tokens, qkv_weight.transpose(1, 2, 0), out_weight, prefill_cache[0].transpose(0, 2, 1),
        decode_cache.transpose(0, 1, 3, 2), decode_tokens, attention_gain, feedforward_gain, decode_lengths,
        request_slot, prefill_offsets,
    )
    hidden, dhidden, normed, dnormed = deliver(hidden, dhidden, normed, dnormed)
    return hidden, dhidden, normed, dnormed


def solution(mesh):
    placed = (
        P("seq", None),
        P("seq", None),
        P(),
        P(None, None, "tp"),
        P("tp", None),
        P(),
        P("seq", None, None, "tp"),
        P("seq"),
        P("seq", None, None, "tp"),
        P("seq"),
        P(),
    )
    return jax.shard_map(
        functools.partial(local_step, mesh.shape["seq"]),
        mesh=mesh,
        in_specs=placed,
        out_specs=(P("seq", None), P("seq", None), P("seq", None), P("seq", None)),
        check_vma=False,
    )
```

```python
import functools

import jax
import jax.numpy as jnp
import numpy as np
from jax import lax
from jax.experimental import pallas as pl
from jax.experimental.pallas import tpu as pltpu
from jax.sharding import PartitionSpec as P

HEAD = 64
HALF = HEAD // 2
RMS_EPSILON = 1e-05
ROPE_BASE = 10000.0
NEGATIVE = -1e30
GROUP = 3
PIECE = 64
FREQUENCY = [float(np.float32(ROPE_BASE ** (-2.0 * i / HEAD))) for i in range(HALF)]
MIB = 1 << 20
F32, BF16 = jnp.float32, jnp.bfloat16
MESH = pl.DeviceIdType.MESH
VMEM = pltpu.VMEM
VSPEC = pl.BlockSpec(memory_space=pltpu.VMEM)
HSPEC = pl.BlockSpec(memory_space=pltpu.HBM)
SSPEC = pl.BlockSpec(memory_space=pltpu.SMEM)


def dot(a, b, ca, cb):
    return lax.dot_general(a, b, (((ca,), (cb,)), ((), ())), preferred_element_type=F32)


def rms_rows(x, gain):
    inverse = lax.rsqrt(jnp.mean(x * x, axis=-1, keepdims=True) + RMS_EPSILON)
    return (x * inverse * gain).astype(BF16)


def rotate_columns(x, cosine, sine, scale):
    pieces = []
    for head in range(x.shape[0] // HEAD):
        a = x[head * HEAD : head * HEAD + HALF]
        b = x[head * HEAD + HALF : (head + 1) * HEAD]
        pieces.append(a * cosine - b * sine)
        pieces.append(b * cosine + a * sine)
    turned = jnp.concatenate(pieces, axis=0).astype(BF16)
    return turned if scale is None else (turned.astype(F32) * scale).astype(BF16)


def block_kernel(
    n, chunks, tok_hbm, wqkv_hbm, wo_hbm, pcache_hbm, dcache_hbm, dtok_hbm, gain_hbm, gain2_hbm,
    length_hbm, slot_hbm, offset_ref,
    hid_ref, dhid_ref, nor_ref, dnor_ref,
    tok, wqkv, wo, pcache, dcache, dtok, gain, gain2, lengths, slot,
    normed, proj, arrived, results, routed, part, got1, pair, got2, dpart, dgot1, dpair, dgot2, dhalf,
    load_sem, send1, recv1, send2, recv2, s1, r1, s2, r2, s3, r3,
):
    rows, width = tok.shape
    slots = dhid_ref.shape[0]
    local = wo.shape[0]
    heads = local // HEAD
    wide = GROUP * HEAD
    pieces = rows // PIECE
    own_rows = PIECE // 2
    half_width = width // 2
    keys = pcache.shape[2]
    dkeys = dcache.shape[3]
    half = rows // 2
    seq = lax.axis_index("seq")
    tp = lax.axis_index("tp")
    side = lax.rem(tp, 2)
    core = tp + 1 - 2 * side
    across = lax.rem(tp + 2, 4)
    mine = pl.multiple_of(side * own_rows, own_rows)
    other = pl.multiple_of((1 - side) * own_rows, own_rows)

    pairs = (
        (length_hbm, lengths),
        (gain_hbm, gain),
        (dtok_hbm, dtok),
        (gain2_hbm, gain2),
        (slot_hbm, slot),
        (tok_hbm.at[:half], tok.at[:half]),
        (wqkv_hbm.at[0], wqkv.at[0]),
        (wqkv_hbm.at[1], wqkv.at[1]),
        (wqkv_hbm.at[2], wqkv.at[2]),
        (pcache_hbm.at[0], pcache.at[0]),
        (pcache_hbm.at[1], pcache.at[1]),
        (wo_hbm, wo),
        (tok_hbm.at[half:], tok.at[half:]),
        (dcache_hbm, dcache),
    )
    loads = [pltpu.make_async_copy(src, dst, load_sem.at[i]) for i, (src, dst) in enumerate(pairs)]
    smalls, loads = loads[:5], loads[5:]
    for load in smalls[:2] + loads[:4]:
        load.start()

    barrier = pltpu.get_barrier_semaphore()
    for step in range(1, n):
        pl.semaphore_signal(barrier, inc=1, device_id={"seq": lax.rem(seq + step, n)}, device_id_type=MESH)
    for step in range(1, 4):
        pl.semaphore_signal(barrier, inc=1, device_id={"tp": lax.rem(tp + step, 4)}, device_id_type=MESH)

    def spread(buffer, send, recv):
        return [
            pltpu.make_async_remote_copy(
                src_ref=buffer.at[seq],
                dst_ref=buffer.at[seq],
                send_sem=send.at[step],
                recv_sem=recv.at[step],
                device_id={"seq": lax.rem(seq + step, n)},
                device_id_type=MESH,
            )
            for step in range(1, n)
        ]

    def send(src, dst, ssem, rsem, to):
        return pltpu.make_async_remote_copy(
            src_ref=src, dst_ref=dst, send_sem=ssem, recv_sem=rsem,
            device_id={"tp": to}, device_id_type=MESH,
        )

    def owned(c):
        return pl.ds(c * PIECE + mine, own_rows)

    def others(c):
        return pl.ds(c * PIECE + other, own_rows)

    there = spread(arrived, send1, recv1)
    back = spread(results, send2, recv2)
    first = [
        send(part.at[c, pl.ds(other, own_rows)], got1.at[c], s1.at[c], r1.at[c], core) for c in range(pieces)
    ] + [send(dpart.at[1 - side], dgot1, s1.at[pieces], r1.at[pieces], core)]
    second = [send(pair.at[c], got2.at[c], s2.at[c], r2.at[c], across) for c in range(pieces)] + [
        send(dpair, dgot2, s2.at[pieces], r2.at[pieces], across)
    ]
    third = [send(hid_ref.at[owned(c)], hid_ref.at[owned(c)], s3.at[c], r3.at[c], core) for c in range(pieces)] + [
        send(dhalf.at[side], dhalf.at[side], s3.at[pieces], r3.at[pieces], core)
    ]

    row = lax.broadcasted_iota(jnp.int32, (HALF, 1), 0)
    frequency = jnp.zeros((HALF, 1), F32)
    for i, value in enumerate(FREQUENCY):
        frequency = jnp.where(row == i, value, frequency)
    angles = frequency * (offset_ref[0].astype(F32) + lax.broadcasted_iota(jnp.int32, (1, rows), 1).astype(F32))
    cosine, sine = jnp.cos(angles), jnp.sin(angles)
    bias = jnp.where(lax.broadcasted_iota(jnp.int32, (1, keys), 1) < offset_ref[0], 0.0, NEGATIVE)
    smalls[0].wait()
    length = lengths[...].reshape(1, slots).astype(F32)
    dangles = frequency * length
    dcos, dsin = jnp.cos(dangles), jnp.sin(dangles)

    smalls[1].wait()
    scale1 = gain[...].reshape(1, width)

    def norm_rows(start, stop):
        for low in range(start, stop, 64):
            normed[low - start : low - start + 64, :] = rms_rows(tok[low : low + 64, :].astype(F32), scale1)

    def project(index, start, stop):
        product = dot(wqkv[index], normed[...], 1, 1).astype(BF16)
        if index < 2:
            product = rotate_columns(
                product.astype(F32), cosine[:, start:stop], sine[:, start:stop], 0.125 if index == 0 else None
            )
        proj[index, :, start:stop] = product

    def attend(start, stop):
        chunk = stop - start
        causal = lax.broadcasted_iota(jnp.int32, (GROUP * chunk, chunk), 1) <= lax.rem(
            lax.broadcasted_iota(jnp.int32, (GROUP * chunk, chunk), 0), chunk
        )
        block = lax.broadcasted_iota(jnp.int32, (chunk, wide), 1) // HEAD
        mixes = []
        for group in range(heads // GROUP):
            span = slice(group * wide, (group + 1) * wide)
            turned = proj[0, span, start:stop].astype(F32).T
            query = jnp.concatenate(
                [jnp.where(block == i, turned, 0.0).astype(BF16) for i in range(GROUP)], axis=0
            )
            scores = [dot(query, pcache[0, span, :], 1, 0) + bias]
            scores.append(jnp.where(causal, dot(query, proj[1, span, start:stop], 1, 0), NEGATIVE))
            values = [pcache[1, span, :], proj[2, span, start:stop]]
            if start > 0:
                scores.append(dot(query, proj[1, span, :start], 1, 0))
                values.append(proj[2, span, :start])
            peak = functools.reduce(jnp.maximum, [jnp.max(x, axis=-1, keepdims=True) for x in scores])
            exps = [jnp.exp(x - peak) for x in scores]
            total = functools.reduce(jnp.add, [jnp.sum(x, axis=-1, keepdims=True) for x in exps])
            mixed = functools.reduce(
                jnp.add, [dot(x.astype(BF16), v, 1, 1) for x, v in zip(exps, values)]
            ) * (1.0 / total)
            own = mixed[:chunk]
            for i in range(1, GROUP):
                own = jnp.where(block == i, mixed[i * chunk : (i + 1) * chunk], own)
            mixes.append(own.astype(BF16))
        out = functools.reduce(
            jnp.add, [dot(x, wo[g * wide : (g + 1) * wide, :], 1, 0) for g, x in enumerate(mixes)]
        ).astype(BF16)
        for low in range(start, stop, PIECE):
            c = low // PIECE
            part[c] = out[low - start : low - start + PIECE]

    def launch(*cs):
        for c in cs:
            first[c].start()

    def cross(*cs):
        for c in cs:
            first[c].wait_recv()
        for c in cs:
            if c < pieces:
                pair[c] = (part[c, pl.ds(mine, own_rows)].astype(F32) + got1[c].astype(F32)).astype(BF16)
            else:
                dpair[...] = (dpart[side].astype(F32) + dgot1[...].astype(F32)).astype(BF16)
        for c in cs:
            second[c].start()

    def finish(*cs):
        for c in cs:
            second[c].wait_recv()
        for c in cs:
            if c < pieces:
                combined = pair[c].astype(F32) + got2[c].astype(F32)
                hid_ref[owned(c), :] = (tok[owned(c), :].astype(F32) + combined).astype(BF16)
            else:
                combined = dpair[...].astype(F32) + dgot2[...].astype(F32)
                tokens = jnp.where(
                    side == 0, dtok[:, :half_width].astype(F32), dtok[:, half_width:].astype(F32)
                )
                dhalf[side] = (tokens + combined).astype(BF16)
        for c in cs:
            third[c].start()

    def settle(*cs):
        for c in cs:
            third[c].wait_recv()
        for c in cs:
            if c < pieces:
                span = slice(c * PIECE, (c + 1) * PIECE)
                nor_ref[span, :] = rms_rows(hid_ref[span, :].astype(F32), scale2)
            else:
                hidden = jnp.concatenate([dhalf[0], dhalf[1]], axis=1)
                dhid_ref[...] = hidden
                dnor_ref[...] = rms_rows(hidden.astype(F32), scale2)

    loads[0].wait()
    norm_rows(0, half)
    for load in loads[4:6]:
        load.start()
    loads[1].wait()
    project(0, 0, half)
    for load in loads[6:8] + smalls[2:]:
        load.start()
    loads[2].wait()
    project(1, 0, half)
    loads[8].start()
    loads[3].wait()
    project(2, 0, half)
    for load in loads[4:7]:
        load.wait()
    pl.semaphore_wait(barrier, n + 2)
    attend(*chunks[0])
    launch(0, 1)

    for load in smalls[2:]:
        load.wait()
    scale2 = gain2[...].reshape(1, width)
    dnormed = rms_rows(dtok[...].astype(F32), scale1)
    for index in range(3):
        arrived[seq, index] = dot(dnormed, wqkv[index], 1, 1).astype(BF16)
    for copy in there:
        copy.start()
    cross(0, 1)
    attend(*chunks[1])
    launch(2, 3)
    loads[7].wait()
    norm_rows(half, rows)
    project(0, half, rows)
    cross(2, 3)
    project(1, half, rows)
    project(2, half, rows)
    attend(*chunks[2])
    launch(4, 5)

    for copy in there:
        copy.wait()
    loads[8].wait()
    total = n * slots
    chosen = seq * slots + lax.broadcasted_iota(jnp.int32, (slots, total), 0)
    slot_row = slot[...].reshape(1, total)
    pick = (slot_row == chosen).astype(F32).astype(BF16)
    placing = (slot_row == lax.broadcasted_iota(jnp.int32, (total, total), 0)).astype(F32).astype(BF16)

    def gathered(which):
        return arrived[:, which].astype(F32).reshape(total, local).astype(BF16)

    q = rotate_columns(dot(gathered(0), pick, 0, 1).astype(BF16).astype(F32), dcos, dsin, 0.125).astype(F32)
    k = rotate_columns(dot(gathered(1), pick, 0, 1).astype(BF16).astype(F32), dcos, dsin, None).astype(F32)
    v = dot(pick, gathered(2), 1, 0).astype(BF16).astype(F32)
    cross(4, 5)
    finish(0, 1)

    padded = 16
    own_head = (
        lax.broadcasted_iota(jnp.int32, (local, padded), 0) // HEAD
        == lax.broadcasted_iota(jnp.int32, (local, padded), 1)
    )
    own_lane = (
        lax.broadcasted_iota(jnp.int32, (padded, local), 1) // HEAD
        == lax.broadcasted_iota(jnp.int32, (padded, local), 0)
    )
    position = lax.broadcasted_iota(jnp.int32, (1, dkeys), 1).astype(F32)
    product = q * k
    own = jnp.concatenate(
        [
            jnp.sum(product[head * HEAD : (head + 1) * HEAD], axis=0, keepdims=True)
            if head < heads
            else jnp.zeros((1, slots), F32)
            for head in range(padded)
        ],
        axis=0,
    )
    own = jnp.concatenate([own[:, s : s + 1] for s in range(slots)], axis=0)
    scores = []
    for s in range(slots):
        query = jnp.where(own_head, q[:, s : s + 1], 0.0).astype(BF16)
        hidden_keys = jnp.where(position < length[:, s : s + 1], 0.0, NEGATIVE)
        scores.append(dot(query, dcache[s, 0], 0, 0) + hidden_keys)
    scores = jnp.concatenate(scores, axis=0)
    peak = jnp.maximum(jnp.max(scores, axis=-1, keepdims=True), own)
    exps = jnp.exp(scores - peak)
    own_exp = jnp.exp(own - peak)
    denominator = jnp.sum(exps, axis=-1, keepdims=True) + own_exp
    weights = (exps / denominator).astype(BF16)
    own_weight = (own_exp / denominator).astype(BF16).astype(F32)
    attended = []
    for s in range(slots):
        span = slice(s * padded, (s + 1) * padded)
        mixed = dot(weights[span], dcache[s, 1], 1, 1) + own_weight[span] * v[s : s + 1]
        attended.append(jnp.sum(jnp.where(own_lane, mixed, 0.0), axis=0, keepdims=True))
    results[seq] = jnp.concatenate(attended, axis=0).astype(BF16)
    attend(*chunks[3])
    launch(6, 7)
    for copy in back:
        copy.start()
    settle(0, 1)
    finish(2, 3)
    cross(6, 7)
    settle(2, 3)
    for copy in back:
        copy.wait()
    every = results[...].astype(F32).reshape(total, local).astype(BF16)
    routed[...] = dot(placing, every, 0, 0)
    returned = routed[pl.ds(pl.multiple_of(seq * slots, slots), slots), :].astype(BF16)
    mixed = dot(returned, wo[...], 1, 0).astype(BF16)
    dpart[0] = mixed[:, :half_width]
    dpart[1] = mixed[:, half_width:]
    launch(pieces)
    finish(4)
    cross(pieces)
    finish(5)
    settle(4, 5)
    finish(pieces, 6)
    settle(pieces, 6)
    finish(7)
    settle(7)
    for copy in first + second + third:
        copy.wait_send()


def block(n, tokens, wqkv, wo, pcache, dcache, dtokens, gain, gain2, lengths, slot, offset):
    rows, width = tokens.shape
    slots = dtokens.shape[0]
    local = wo.shape[0]
    pieces = rows // PIECE
    chunks = ((0, 128), (128, 256), (256, 384), (384, 512))
    buffer = VMEM((pieces, PIECE // 2, width), BF16)
    dbuffer = VMEM((slots, width // 2), BF16)
    dhalves = VMEM((2, slots, width // 2), BF16)
    sem = pltpu.SemaphoreType.DMA((pieces + 1,))
    args = (tokens, wqkv, wo, pcache, dcache, dtokens, gain, gain2, lengths, slot)
    args = [pltpu.with_memory_space_constraint(x, pltpu.HBM) for x in args]
    return pl.pallas_call(
        functools.partial(block_kernel, n, chunks),
        in_specs=[HSPEC] * 10 + [SSPEC],
        out_specs=[VSPEC] * 4,
        out_shape=[jax.ShapeDtypeStruct((x, width), BF16) for x in (rows, slots, rows, slots)],
        scratch_shapes=[VMEM(x.shape, x.dtype) for x in args]
        + [
            VMEM((rows // 2, width), BF16),
            VMEM((3, local, rows), BF16),
            VMEM((n, 3, slots, local), BF16),
            VMEM((n, slots, local), BF16),
            VMEM((n * slots, local), F32),
            VMEM((pieces, PIECE, width), BF16),
            buffer, buffer, buffer,
            dhalves, dbuffer, dbuffer, dbuffer, dhalves,
            pltpu.SemaphoreType.DMA((14,)),
        ]
        + [pltpu.SemaphoreType.DMA((n,))] * 4
        + [sem] * 6,
        compiler_params=pltpu.CompilerParams(
            collective_id=0, has_side_effects=True, vmem_limit_bytes=44 * MIB
        ),
        name="block",
    )(*args, offset)


def deliver_kernel(hid, dhid, nor, dnor, hid_out, dhid_out, nor_out, dnor_out, sem):
    rows = hid.shape[0]
    step = rows // 4
    copies = []
    for src, dst in ((hid, hid_out), (nor, nor_out)):
        for i in range(4):
            span = pl.ds(i * step, step)
            copies.append((src.at[span], dst.at[span]))
    copies += [(dhid, dhid_out), (dnor, dnor_out)]
    copies = [pltpu.make_async_copy(src, dst, sem.at[i]) for i, (src, dst) in enumerate(copies)]
    for copy in copies:
        copy.start()
    for copy in copies:
        copy.wait()


def deliver(*arrays):
    return pl.pallas_call(
        deliver_kernel,
        in_specs=[VSPEC] * 4,
        out_specs=[HSPEC] * 4,
        out_shape=[jax.ShapeDtypeStruct(x.shape, BF16) for x in arrays],
        scratch_shapes=[pltpu.SemaphoreType.DMA((10,))],
        compiler_params=pltpu.CompilerParams(vmem_limit_bytes=16 * MIB),
        name="deliver",
    )(*arrays)


def local_step(
    n,
    prefill_tokens,
    decode_tokens,
    attention_gain,
    qkv_weight,
    out_weight,
    feedforward_gain,
    prefill_cache,
    prefill_offsets,
    decode_cache,
    decode_lengths,
    request_slot,
):
    hidden, dhidden, normed, dnormed = block(
        n, prefill_tokens, qkv_weight.transpose(1, 2, 0), out_weight, prefill_cache[0].transpose(0, 2, 1),
        decode_cache.transpose(0, 1, 3, 2), decode_tokens, attention_gain, feedforward_gain, decode_lengths,
        request_slot, prefill_offsets,
    )
    hidden, dhidden, normed, dnormed = deliver(hidden, dhidden, normed, dnormed)
    return hidden, dhidden, normed, dnormed


def solution(mesh):
    placed = (
        P("seq", None),
        P("seq", None),
        P(),
        P(None, None, "tp"),
        P("tp", None),
        P(),
        P("seq", None, None, "tp"),
        P("seq"),
        P("seq", None, None, "tp"),
        P("seq"),
        P(),
    )
    return jax.shard_map(
        functools.partial(local_step, mesh.shape["seq"]),
        mesh=mesh,
        in_specs=placed,
        out_specs=(P("seq", None), P("seq", None), P("seq", None), P("seq", None)),
        check_vma=False,
    )
```
